256 devices in a mesh: dp: 32 (over y_lo, z, core), ctx: 8 (over y_hi, x).
Axes of the slice: x: 4, y: 4 (y_hi: 2, y_lo: 2; y = y_hi * 2 + y_lo), z: 8, core: 2. Of those that a mesh axis runs over, the one named last changes fastest.
Arguments:
- normed_input: bfloat16 [32768, 4096], P(('dp', 'ctx')), may hold values from -24 to 24
- queries: bfloat16 [32768, 4096], P(('dp', 'ctx')), may hold values from -120 to 120
- saved_keys: bfloat16 [32768, 512], P(('dp', 'ctx')), may hold values from -6 to 6
- saved_values: bfloat16 [32768, 512], P(('dp', 'ctx')), may hold values from -6 to 6
- attention_output: bfloat16 [32768, 4096], P(('dp', 'ctx')), may hold values from -6 to 6, as said below
- saved_log_totals: float32 [32768, 32], P(('dp', 'ctx')), as said below
- output_gradient: bfloat16 [32768, 4096], P(('dp', 'ctx')), may hold values from -6 to 6
- document_lengths: int32 [32, 4], P('dp'), may hold values from 1 to 512, as said below
Outputs:
- query_gradient: bfloat16 [32768, 4096], P(('dp', 'ctx'))
- key_weight_grad: float32 [4096, 512], P(('dp', 'ctx'))
- value_weight_grad: float32 [4096, 512], P(('dp', 'ctx'))
The draws below stay inside these ranges and needn't reach their ends.
Inputs may be any that keep to these rules, and one draw needn't show every extreme that they name: `document_lengths`: each sequence holds 4 documents whose lengths sum to 1024; the longest is exactly 512. attention_output is the forward's output, the softmax over allowed keys of the scores applied to saved_values, for the given queries, saved_keys, saved_values and document_lengths, rounded to bfloat16. saved_log_totals is the log of the sum of exp of the allowed scores of each query row and head, for the given queries, saved_keys and document_lengths.
All inputs are finite; a program needn't handle non-finite values.
Results may differ from the reference program's by a relative error of at most 0.0051.
Values may be sent and summed in bfloat16 or wider, within the bound.
A program may use at most 128 MiB of HBM per device.

```python
import math
import jax
import jax.numpy as jnp
from jax import lax

D = 4096
QUERY_HEADS = 32
KEY_VALUE_HEADS = 4
HEAD_SIZE = 128
TOK_DEV = 128
NDOCS = 4
SEQUENCE_LENGTH = 1024
MOST = 512
SEQUENCE_COUNT = 32
TOKEN_COUNT = 32768
N_CTX = 8


def drawn_parts(key):
    start_offset = jnp.clip(jax.random.normal(jax.random.fold_in(key, 11), (TOKEN_COUNT, KEY_VALUE_HEADS * HEAD_SIZE), jnp.float32), -6.0, 6.0)
    return start_offset


def query_floats(key):
    return jnp.clip(jax.random.normal(jax.random.fold_in(key, 15), (TOKEN_COUNT, QUERY_HEADS * HEAD_SIZE), jnp.float32), -6.0, 6.0)


def key_floats(key):
    start_offset = drawn_parts(key)
    return start_offset


def value_floats(key):
    return jnp.clip(jax.random.normal(jax.random.fold_in(key, 16), (TOKEN_COUNT, KEY_VALUE_HEADS * HEAD_SIZE), jnp.float32), -6.0, 6.0)


def draw_queries(key, part):
    return query_floats(key).astype(jnp.bfloat16)


def draw_saved_keys(key, part):
    return key_floats(key).astype(jnp.bfloat16)


def draw_saved_values(key, part):
    return value_floats(key).astype(jnp.bfloat16)


def draw_document_lengths(key, part):
    rest = SEQUENCE_LENGTH - MOST

    def one_row(row_key):
        cut_key, slot_key = jax.random.split(row_key)
        cuts = jnp.sort(jax.random.permutation(cut_key, rest - 1)[:NDOCS - 2].astype(jnp.int32) + 1)
        bounds = jnp.concatenate([jnp.zeros((1,), jnp.int32), cuts, jnp.full((1,), rest, jnp.int32)])
        pieces = bounds[1:] - bounds[:-1]
        slot = jax.random.randint(slot_key, (), 0, NDOCS)
        index = jnp.arange(NDOCS, dtype=jnp.int32)
        before = pieces[jnp.clip(index, 0, NDOCS - 2)]
        after = pieces[jnp.clip(index - 1, 0, NDOCS - 2)]
        return jnp.where(index == slot, jnp.int32(MOST), jnp.where(index < slot, before, after)).astype(jnp.int32)
    return jax.vmap(one_row)(jax.random.split(jax.random.fold_in(key, 21), SEQUENCE_COUNT))


def forward_pass(key):
    group_count = QUERY_HEADS // KEY_VALUE_HEADS
    softmax_scale = 1.0 / math.sqrt(HEAD_SIZE)
    query_all = query_floats(key).astype(jnp.bfloat16).astype(jnp.float32).reshape(SEQUENCE_COUNT, SEQUENCE_LENGTH, QUERY_HEADS * HEAD_SIZE)
    key_all = key_floats(key).astype(jnp.bfloat16).astype(jnp.float32).reshape(SEQUENCE_COUNT, SEQUENCE_LENGTH, KEY_VALUE_HEADS * HEAD_SIZE)
    value_all = value_floats(key).astype(jnp.bfloat16).astype(jnp.float32).reshape(SEQUENCE_COUNT, SEQUENCE_LENGTH, KEY_VALUE_HEADS * HEAD_SIZE)
    lengths = draw_document_lengths(key, 0)

    def one_sequence(operand_list):
        query_row_matrix, key_row_matrix, value_row_matrix, lengths_row = operand_list
        row_ids = jnp.arange(SEQUENCE_LENGTH, dtype=jnp.int32)
        positions = row_ids % TOK_DEV * N_CTX + row_ids // TOK_DEV
        doc_ends = jnp.cumsum(lengths_row)
        documents = jnp.sum((doc_ends[None, :] <= positions[:, None]).astype(jnp.int32), axis=1)
        allowed = (documents[:, None] == documents[None, :]) & (positions[None, :] <= positions[:, None])
        score_matrix = jnp.einsum('szot,mzt->zosm', query_row_matrix.reshape(SEQUENCE_LENGTH, KEY_VALUE_HEADS, group_count, HEAD_SIZE), key_row_matrix.reshape(SEQUENCE_LENGTH, KEY_VALUE_HEADS, HEAD_SIZE), precision=lax.Precision.HIGHEST) * softmax_scale
        score_matrix = jnp.where(allowed, score_matrix, -1e+30)
        row_max = jnp.max(score_matrix, axis=-1, keepdims=True)
        attention_weights = jnp.where(allowed, jnp.exp(score_matrix - row_max), 0.0)
        softmax_totals = jnp.sum(attention_weights, axis=-1, keepdims=True)
        attended_output = jnp.einsum('sjba,asp->bsjp', attention_weights / softmax_totals, value_row_matrix.reshape(SEQUENCE_LENGTH, KEY_VALUE_HEADS, HEAD_SIZE), precision=lax.Precision.HIGHEST)
        log_softmax_total = jnp.transpose((row_max + jnp.log(softmax_totals))[..., 0], (2, 0, 1))
        return (log_softmax_total.reshape(SEQUENCE_LENGTH, QUERY_HEADS), attended_output.reshape(SEQUENCE_LENGTH, QUERY_HEADS * HEAD_SIZE))
    return lax.map(one_sequence, (query_all, key_all, value_all, lengths))


def draw_saved_log_totals(key, part):
    return forward_pass(key)[0].reshape(TOKEN_COUNT, QUERY_HEADS).astype(jnp.float32)


def draw_attention_output(key, part):
    return forward_pass(key)[1].reshape(TOKEN_COUNT, QUERY_HEADS * HEAD_SIZE).astype(jnp.bfloat16)


def spiked(result, own_key, source, target, blocks, factor):
    def block_of(axis_at):
        return (jnp.arange(result.shape[axis_at]) // (result.shape[axis_at] // blocks)).reshape((-1,) + (1,) * (result.ndim - 1 - axis_at))

    first = jax.random.permutation(own_key, blocks)[block_of(target)]
    second = (block_of(target) + blocks // 2) % blocks
    return jnp.where((block_of(source) == first) | (block_of(source) == second), factor * result, result)


def levels(rng, extent, cuts, smallest, top_value):
    def one(dim, parts):
        draws = jax.random.uniform(jax.random.fold_in(jax.random.fold_in(rng, 6), dim), (parts,), jnp.float32, smallest / len(cuts), top_value / len(cuts))
        return jnp.repeat(jnp.exp(draws), extent[dim] // parts).reshape((-1,) + (1,) * (len(extent) - dim - 1))

    loudness = one(*cuts[0])
    for cut in cuts[1:]:
        loudness = loudness * one(*cut)
    return loudness


def gaussian(stream_key, extent, width, reach, cuts=(), kind=jnp.bfloat16):
    entries = width * jax.random.normal(stream_key, extent, jnp.float32)
    if cuts:
        entries = entries * levels(stream_key, extent, cuts, -0.22, 0.18)
    return jnp.clip(entries, -reach, reach).astype(kind)


def gaussian_with(stream_key, dims, spread, bound, cuts, heavy, held_as=jnp.bfloat16):
    result = spread * jax.random.normal(stream_key, dims, jnp.float32)
    if cuts:
        result = result * levels(stream_key, dims, cuts, -0.22, 0.18)
    return jnp.clip(spiked(result, jax.random.fold_in(stream_key, 3), *heavy), -bound, bound).astype(held_as)


def setup_inputs(seed: int = 0) -> dict:
    keys = jax.random.split(jax.random.key(seed), 9)
    normed_input = gaussian_with(keys[0], (TOKEN_COUNT, D), 1.0, 24.0, ((0, 256),), (0, 1, 256, 6.0))
    queries = draw_queries(jax.random.fold_in(keys[8], 71), 0)
    saved_keys = draw_saved_keys(jax.random.fold_in(keys[8], 71), 0)
    saved_values = draw_saved_values(jax.random.fold_in(keys[8], 71), 0)
    attention_output = draw_attention_output(jax.random.fold_in(keys[8], 71), 0)
    saved_log_totals = draw_saved_log_totals(jax.random.fold_in(keys[8], 71), 0)
    output_gradient = gaussian(keys[6], (TOKEN_COUNT, QUERY_HEADS * HEAD_SIZE), 1.0, 6.0, ((0, 256),))
    document_lengths = draw_document_lengths(jax.random.fold_in(keys[8], 71), 0)
    return dict(normed_input=normed_input, queries=queries, saved_keys=saved_keys, saved_values=saved_values, attention_output=attention_output, saved_log_totals=saved_log_totals, output_gradient=output_gradient, document_lengths=document_lengths)


highest = lax.Precision.HIGHEST

def doc_index(lengths_row, positions):
    doc_ends = jnp.cumsum(lengths_row)
    return lax.optimization_barrier(jnp.sum((doc_ends[None, :] <= positions[:, None]).astype(jnp.int32), axis=1))

def one_sequence(operand_list):
    queries, saved_keys, saved_values, attention_output, saved_log_totals, output_gradient, lengths_row = operand_list
    group_count = QUERY_HEADS // KEY_VALUE_HEADS
    softmax_scale = 1.0 / math.sqrt(HEAD_SIZE)
    row_ids = jnp.arange(SEQUENCE_LENGTH, dtype=jnp.int32)
    positions = row_ids % TOK_DEV * N_CTX + row_ids // TOK_DEV
    documents = doc_index(lengths_row, positions)
    allowed = (documents[:, None] == documents[None, :]) & (positions[None, :] <= positions[:, None])
    query_tensor_four = queries.reshape(SEQUENCE_LENGTH, KEY_VALUE_HEADS, group_count, HEAD_SIZE).astype(jnp.float32)
    key_tensor_three = saved_keys.reshape(SEQUENCE_LENGTH, KEY_VALUE_HEADS, HEAD_SIZE).astype(jnp.float32)
    value_tensor_three = saved_values.reshape(SEQUENCE_LENGTH, KEY_VALUE_HEADS, HEAD_SIZE).astype(jnp.float32)
    output_gradient_four = output_gradient.reshape(SEQUENCE_LENGTH, KEY_VALUE_HEADS, group_count, HEAD_SIZE).astype(jnp.float32)
    output_tensor_four = attention_output.reshape(SEQUENCE_LENGTH, KEY_VALUE_HEADS, group_count, HEAD_SIZE).astype(jnp.float32)
    log_softmax_total = jnp.transpose(saved_log_totals.reshape(SEQUENCE_LENGTH, KEY_VALUE_HEADS, group_count), (1, 2, 0))
    score_matrix = jnp.einsum('szot,mzt->zosm', query_tensor_four, key_tensor_three, precision=highest) * softmax_scale
    probs = jnp.where(allowed, jnp.exp(score_matrix - log_softmax_total[..., None]), 0.0)
    delta_row = jnp.transpose(lax.optimization_barrier(jnp.sum(output_gradient_four * output_tensor_four, axis=-1)), (1, 2, 0))
    grad_probs = jnp.einsum('szot,mzt->zosm', output_gradient_four, value_tensor_three, precision=highest)
    grad_scores = lax.optimization_barrier((probs * (grad_probs - delta_row[..., None])).astype(jnp.bfloat16)).astype(jnp.float32)
    probs_low = lax.optimization_barrier(probs.astype(jnp.bfloat16)).astype(jnp.float32)
    grad_query = softmax_scale * jnp.einsum('sjba,asp->bsjp', grad_scores, key_tensor_three, precision=highest)
    key_gradient = softmax_scale * jnp.einsum('hgqk,qhgd->khd', grad_scores, query_tensor_four, precision=highest)
    value_gradient = jnp.einsum('hgqk,qhgd->khd', probs_low, output_gradient_four, precision=highest)
    key_value_gradients = jnp.concatenate([key_gradient.reshape(SEQUENCE_LENGTH, KEY_VALUE_HEADS * HEAD_SIZE), value_gradient.reshape(SEQUENCE_LENGTH, KEY_VALUE_HEADS * HEAD_SIZE)], axis=1)
    return (grad_query.reshape(SEQUENCE_LENGTH, QUERY_HEADS * HEAD_SIZE).astype(jnp.bfloat16), key_value_gradients.astype(jnp.bfloat16))

def reference(normed_input, queries, saved_keys, saved_values, attention_output, saved_log_totals, output_gradient, document_lengths):
    operand_list = (queries.reshape(SEQUENCE_COUNT, SEQUENCE_LENGTH, QUERY_HEADS * HEAD_SIZE), saved_keys.reshape(SEQUENCE_COUNT, SEQUENCE_LENGTH, KEY_VALUE_HEADS * HEAD_SIZE), saved_values.reshape(SEQUENCE_COUNT, SEQUENCE_LENGTH, KEY_VALUE_HEADS * HEAD_SIZE), attention_output.reshape(SEQUENCE_COUNT, SEQUENCE_LENGTH, QUERY_HEADS * HEAD_SIZE), saved_log_totals.reshape(SEQUENCE_COUNT, SEQUENCE_LENGTH, QUERY_HEADS), output_gradient.reshape(SEQUENCE_COUNT, SEQUENCE_LENGTH, QUERY_HEADS * HEAD_SIZE), document_lengths)
    query_gradient, key_value_gradients = lax.map(one_sequence, operand_list)
    query_gradient = query_gradient.reshape(TOKEN_COUNT, QUERY_HEADS * HEAD_SIZE)
    key_value_gradients = key_value_gradients.reshape(TOKEN_COUNT, 2 * KEY_VALUE_HEADS * HEAD_SIZE)
    weight_gradient = jnp.dot(normed_input.T, key_value_gradients, preferred_element_type=jnp.float32)
    return (query_gradient, weight_gradient[:, :KEY_VALUE_HEADS * HEAD_SIZE], weight_gradient[:, KEY_VALUE_HEADS * HEAD_SIZE:])
```

```python
import math

import jax
import jax.numpy as jnp
from jax import lax
from jax.experimental import pallas as pl
from jax.experimental.pallas import tpu as pltpu
from jax.sharding import PartitionSpec as P

KV_HEADS = 4
GROUP = 8
HEADS = KV_HEADS * GROUP
HEAD = 128
ROWS = 128
CTX = 8
DP = 32
Z = 8
OUT_ROWS = 16
KEYS = 256
SCALE = 1.0 / math.sqrt(HEAD)
LOG2E = math.log2(math.e)
MESH = pl.DeviceIdType.MESH
F32, BF16 = jnp.float32, jnp.bfloat16


def wait_for(ref, sem):
    pltpu.make_async_copy(ref, ref, sem).wait()


def dot(a, b, contract):
    return lax.dot_general(a, b, ((contract[:1], contract[1:]), ((), ())), preferred_element_type=F32)


def kernel(
    x_in, q_in, k_in, v_in, o_in, lse_in, do_in, len_in,
    dq_out, kw_out, vw_out,
    lens, lse, delta, q, do, o, x, xt, xall, kv, bias, pt, dst, dqt, part, parts, grads, w,
    c_land, acc, y_out, y_land, z_out, z_land,
    in_sem, kv_send, kv_recv, x_send, x_recv, p_send, p_recv, g_send, g_recv, d_send, d_recv,
):
    dp, ctx = lax.axis_index("dp"), lax.axis_index("ctx")
    y_hi, cx = ctx // 4, ctx % 4
    y_lo, z, core = dp // (2 * Z), dp // 2 % Z, dp % 2

    def ahead(s):
        return (y_hi + s // 4) % 2 * 4 + (cx + s % 4) % 4

    def behind(s):
        return (y_hi + 2 - s // 4) % 2 * 4 + (cx + 4 - s % 4) % 4

    def z_peer(s):
        return (y_lo * Z + (z + s) % Z) * 2 + core

    core_peer = (y_lo * Z + z) * 2 + 1 - core
    y_peer = ((1 - y_lo) * Z + z) * 2 + core

    def remote(src, dst, send, recv, to):
        return pltpu.make_async_remote_copy(src, dst, send, recv, device_id=to, device_id_type=MESH)

    def cols(h):
        return pl.ds(pl.multiple_of(h * HEAD, HEAD), HEAD)

    pltpu.make_async_copy(len_in, lens, in_sem.at[0]).start()
    pltpu.make_async_copy(lse_in, lse, in_sem.at[1]).start()
    pltpu.make_async_copy(x_in, x, in_sem.at[5]).start()
    pltpu.make_async_copy(o_in, o, in_sem.at[4]).start()

    @pl.loop(0, HEADS)
    def _(h):
        pltpu.make_async_copy(do_in.at[:, cols(h)], do.at[h], in_sem.at[3]).start()
        pltpu.make_async_copy(q_in.at[:, cols(h)], q.at[h], in_sem.at[2]).start()

    @pl.loop(0, KV_HEADS)
    def _(g):
        pltpu.make_async_copy(k_in.at[:, cols(g)], kv.at[g, 0, 0], in_sem.at[6]).start()
        pltpu.make_async_copy(v_in.at[:, cols(g)], kv.at[g, 0, 1], in_sem.at[6]).start()

    barrier = pltpu.get_barrier_semaphore()

    @pl.loop(1, CTX)
    def _(s):
        pl.semaphore_signal(barrier, inc=1, device_id=(dp, ahead(s)), device_id_type=MESH)

    @pl.loop(1, Z)
    def _(s):
        pl.semaphore_signal(barrier, inc=1, device_id=(z_peer(s), ctx), device_id_type=MESH)

    for peer in (core_peer, y_peer):
        pl.semaphore_signal(barrier, inc=1, device_id=(peer, ctx), device_id_type=MESH)
    pl.semaphore_wait(barrier, CTX - 1 + Z - 1 + 2)

    wait_for(kv.at[:, 0], in_sem.at[6])

    @pl.loop(0, KV_HEADS)
    def _(g):
        @pl.loop(1, CTX)
        def _(s):
            remote(kv.at[g, 0], kv.at[g, s], kv_send, kv_recv.at[g], (dp, ahead(s))).start()

    wait_for(x, in_sem.at[5])

    @pl.loop(0, DP)
    def _(b):
        xt[b] = jnp.transpose(x[:, cols(b)]).reshape(CTX, OUT_ROWS, ROWS)

    pltpu.make_async_copy(xt.at[:, ctx], xall.at[:, :, 0:ROWS], in_sem.at[7]).start()

    @pl.loop(1, CTX)
    def _(s):
        to = ahead(s)
        remote(xt.at[:, to], xall.at[:, :, cols(s)], x_send, x_recv, (dp, to)).start()

    wait_for(lens, in_sem.at[0])
    end0 = lens[0, 0]
    end1 = end0 + lens[0, 1]
    end2 = end1 + lens[0, 2]
    end3 = end2 + lens[0, 3]
    query_pos = lax.broadcasted_iota(jnp.int32, (ROWS, ROWS), 1) * CTX + ctx
    first = jnp.zeros((ROWS, ROWS), jnp.int32)
    for end in (end0, end1, end2, end3):
        first = jnp.where(query_pos >= end, end, first)

    @pl.loop(0, CTX)
    def _(s):
        key_pos = lax.broadcasted_iota(jnp.int32, (ROWS, ROWS), 0) * CTX + behind(s)
        allowed = (key_pos >= first) & (key_pos <= query_pos)
        bias[s] = jnp.where(allowed, 0.0, -1e30).astype(F32)

    wait_for(lse, in_sem.at[1])
    wait_for(o, in_sem.at[4])
    wait_for(do, in_sem.at[3])
    wait_for(q, in_sem.at[2])

    @pl.loop(0, KV_HEADS)
    def _(g):
        rows = []
        for h in range(GROUP):
            head = g * GROUP + h
            product = do[head].astype(F32) * o[:, cols(head)].astype(F32)
            rows.append(jnp.sum(jnp.transpose(product), axis=0, keepdims=True))
        delta[pl.ds(pl.multiple_of(g * GROUP, GROUP), GROUP), :] = jnp.concatenate(rows, axis=0)

    def attend(g):
        wait_for(kv.at[g, 1:CTX], kv_recv.at[g])
        heads = pl.ds(pl.multiple_of(g * GROUP, GROUP), GROUP)
        log2_totals = lse[heads, :] * LOG2E
        deltas = delta[heads, :]
        dqt[...] = jnp.zeros_like(dqt)

        @pl.loop(0, CTX * ROWS // KEYS)
        def _(t):
            blocks = pl.ds(t * (KEYS // ROWS), KEYS // ROWS)
            keys = kv[g, blocks, 0].reshape(KEYS, HEAD)
            values = kv[g, blocks, 1].reshape(KEYS, HEAD)
            queries = q[heads].reshape(GROUP * ROWS, HEAD)
            out_grads = do[heads].reshape(GROUP * ROWS, HEAD)
            seen = bias[blocks].reshape(KEYS, ROWS)
            scores = dot(keys, queries, (1, 1))
            grad_probs = dot(values, out_grads, (1, 1))
            for h in range(GROUP):
                at = slice(h * ROWS, (h + 1) * ROWS)
                probs = jnp.exp2(scores[:, at] * (SCALE * LOG2E) + (seen - log2_totals[h : h + 1, :]))
                pt[:, at] = probs.astype(BF16)
                dst[:, at] = (probs * (grad_probs[:, at] - deltas[h : h + 1, :])).astype(BF16)
            grad_scores = dst[...]
            dv = dot(pt[...], out_grads, (1, 0))
            dk = dot(grad_scores, queries, (1, 0)) * SCALE
            part[g, blocks, :, 0:HEAD] = dk.astype(BF16).reshape(KEYS // ROWS, ROWS, HEAD)
            part[g, blocks, :, HEAD:] = dv.astype(BF16).reshape(KEYS // ROWS, ROWS, HEAD)
            dqt[...] += dot(keys, grad_scores, (0, 0))

        @pl.loop(1, CTX)
        def _(s):
            remote(part.at[g, s], parts.at[g, s], p_send, p_recv.at[g], (dp, behind(s))).start()

        for h in range(GROUP):
            block = jnp.transpose(dqt[:, h * ROWS : (h + 1) * ROWS]) * SCALE
            dq_out[:, cols(g * GROUP + h)] = block.astype(BF16)

    def gather_sums(g):
        wait_for(parts.at[g, 1:CTX], p_recv.at[g])
        total = part[g, 0].astype(F32)
        for s in range(1, CTX):
            total += parts[g, s].astype(F32)
        grads[g, 0] = total.astype(BF16)

        @pl.loop(1, CTX)
        def _(s):
            remote(grads.at[g, 0], grads.at[g, s], g_send, g_recv.at[g], (dp, ahead(s))).start()

    def weigh(g):
        wait_for(grads.at[g, 1:CTX], g_recv.at[g])
        product = dot(xall[...].reshape(DP * OUT_ROWS, CTX * ROWS), grads[g].reshape(CTX * ROWS, 2 * HEAD), (1, 0))
        at = pl.ds(pl.multiple_of(g * 2 * HEAD, 2 * HEAD), 2 * HEAD)
        w[:, :, :, :, at] = product.reshape(2, Z, 2, OUT_ROWS, 2 * HEAD)

    @pl.loop(0, KV_HEADS + 2)
    def _(step):
        @pl.when(step < KV_HEADS)
        def _():
            attend(step)

        @pl.when((step >= 1) & (step <= KV_HEADS))
        def _():
            gather_sums(step - 1)

        @pl.when(step == 2)
        def _():
            wait_for(xt.at[:, 0], in_sem.at[7])
            wait_for(xall.at[:, :, ROWS:], x_recv)

        @pl.when(step >= 2)
        def _():
            weigh(step - 2)

    to_core = remote(w.at[:, :, 1 - core], c_land, d_send.at[0], d_recv.at[0], (core_peer, ctx))
    to_core.start()
    to_core.wait()
    acc[...] = w[:, :, core] + c_land[...]
    y_out[...] = acc[1 - y_lo].astype(BF16)
    to_y = remote(y_out, y_land, d_send.at[1], d_recv.at[1], (y_peer, ctx))
    to_y.start()
    to_y.wait()
    acc[0] = acc[y_lo] + y_land[...].astype(F32)
    z_out[...] = acc[0].astype(BF16)

    @pl.loop(1, Z)
    def _(s):
        remote(z_out.at[(z + s) % Z], z_land.at[s], d_send.at[2], d_recv.at[2], (z_peer(s), ctx)).start()

    wait_for(z_land.at[1:Z], d_recv.at[2])
    total = acc[0, z]
    for s in range(1, Z):
        total += z_land[s].astype(F32)
    for g in range(KV_HEADS):
        at = slice(g * HEAD, (g + 1) * HEAD)
        kw_out[:, at] = total[:, 2 * g * HEAD : (2 * g + 1) * HEAD]
        vw_out[:, at] = total[:, (2 * g + 1) * HEAD : (2 * g + 2) * HEAD]

    wait_for(kv.at[:, 1:CTX], kv_send)
    wait_for(xall.at[:, :, ROWS:], x_send)
    wait_for(part.at[:, 1:CTX], p_send)
    wait_for(grads.at[:, 1:CTX], g_send)
    wait_for(z_land.at[1:Z], d_send.at[2])


def local(normed_input, queries, keys, values, attention_output, log_totals, output_gradient, lengths):
    dma = pltpu.SemaphoreType.DMA
    vmem = pltpu.VMEM
    return pl.pallas_call(
        kernel,
        out_shape=(
            jax.ShapeDtypeStruct((ROWS, HEADS * HEAD), BF16),
            jax.ShapeDtypeStruct((OUT_ROWS, KV_HEADS * HEAD), F32),
            jax.ShapeDtypeStruct((OUT_ROWS, KV_HEADS * HEAD), F32),
        ),
        in_specs=[pl.BlockSpec(memory_space=pl.ANY)] * 8,
        out_specs=(pl.BlockSpec(memory_space=vmem),) * 3,
        scratch_shapes=[
            pltpu.SMEM((1, 4), jnp.int32),
            vmem((HEADS, ROWS), F32),
            vmem((HEADS, ROWS), F32),
            vmem((HEADS, ROWS, HEAD), BF16),
            vmem((HEADS, ROWS, HEAD), BF16),
            vmem((ROWS, HEADS * HEAD), BF16),
            vmem((ROWS, DP * CTX * OUT_ROWS), BF16),
            vmem((DP, CTX, OUT_ROWS, ROWS), BF16),
            vmem((DP, OUT_ROWS, CTX * ROWS), BF16),
            vmem((KV_HEADS, CTX, 2, ROWS, HEAD), BF16),
            vmem((CTX, ROWS, ROWS), F32),
            vmem((KEYS, GROUP * ROWS), BF16),
            vmem((KEYS, GROUP * ROWS), BF16),
            vmem((HEAD, GROUP * ROWS), F32),
            vmem((KV_HEADS, CTX, ROWS, 2 * HEAD), BF16),
            vmem((KV_HEADS, CTX, ROWS, 2 * HEAD), BF16),
            vmem((KV_HEADS, CTX, ROWS, 2 * HEAD), BF16),
            vmem((2, Z, 2, OUT_ROWS, 2 * KV_HEADS * HEAD), F32),
            vmem((2, Z, OUT_ROWS, 2 * KV_HEADS * HEAD), F32),
            vmem((2, Z, OUT_ROWS, 2 * KV_HEADS * HEAD), F32),
            vmem((Z, OUT_ROWS, 2 * KV_HEADS * HEAD), BF16),
            vmem((Z, OUT_ROWS, 2 * KV_HEADS * HEAD), BF16),
            vmem((Z, OUT_ROWS, 2 * KV_HEADS * HEAD), BF16),
            vmem((Z, OUT_ROWS, 2 * KV_HEADS * HEAD), BF16),
            dma((8,)),
            dma,
            dma((KV_HEADS,)),
            dma,
            dma,
            dma,
            dma((KV_HEADS,)),
            dma,
            dma((KV_HEADS,)),
            dma((3,)),
            dma((3,)),
        ],
        compiler_params=pltpu.CompilerParams(
            collective_id=0, has_side_effects=True, vmem_limit_bytes=56 * 2**20
        ),
    )(normed_input, queries, keys, values, attention_output, log_totals.T, output_gradient, lengths)


def solution(mesh):
    rows = P(("dp", "ctx"), None)
    return jax.shard_map(
        local,
        mesh=mesh,
        in_specs=(rows,) * 7 + (P("dp", None),),
        out_specs=(rows, rows, rows),
        check_vma=False,
    )
```

```python
import math

import jax
import jax.numpy as jnp
from jax import lax
from jax.experimental import pallas as pl
from jax.experimental.pallas import tpu as pltpu
from jax.sharding import PartitionSpec as P

KV_HEADS = 4
GROUP = 8
HEADS = KV_HEADS * GROUP
HEAD = 128
ROWS = 128
CTX = 8
Y_FIRST = 2
DP = 32
LAGS = (1, 2, 3, 3, 4, 5)
Z = 8
OUT_ROWS = 16
KEYS = 256
SCALE = 1.0 / math.sqrt(HEAD)
LOG2E = math.log2(math.e)
MESH = pl.DeviceIdType.MESH
F32, BF16 = jnp.float32, jnp.bfloat16


def wait_for(ref, sem):
    pltpu.make_async_copy(ref, ref, sem).wait()


def dot(a, b, contract):
    return lax.dot_general(a, b, ((contract[:1], contract[1:]), ((), ())), preferred_element_type=F32)


def kernel(
    x_in, q_in, k_in, v_in, o_in, lse_in, do_in, len_in,
    dq_out, kw_out, vw_out,
    lens, lse, delta, q, do, o, x, xt, xall, kv, bias, pt, dst, dqt, part, y_parts, x_parts, mids, owned, grads, w,
    x_acc, x_out, x_land, z_acc, z_out, z_land,
    in_sem, kv_send, kv_recv, xt_send, xt_recv, p_send, p_recv, m_recv, g_send, g_recv, c_recv,
    x_send, x_recv, z_send, z_recv,
):
    dp, ctx = lax.axis_index("dp"), lax.axis_index("ctx")
    y_hi, cx = ctx // 4, ctx % 4
    y_lo, z, core = dp // (2 * Z), dp // 2 % Z, dp % 2
    y = y_hi * 2 + y_lo

    def behind(s):
        return (y_hi + s % 2) % 2 * 4 + (cx + 4 - s // 2) % 4

    y_partner = (dp, (1 - y_hi) * 4 + cx)

    def along_z(s):
        return ((y_lo * Z + (z + s) % Z) * 2 + core, ctx)

    def along_x(s):
        return (dp, y_hi * 4 + (cx + s) % 4)

    def member(s):
        return (core + s // 4) % 2, (y + s % 4) % 4

    def device(its_core, its_y):
        return ((its_y % 2 * Z + z) * 2 + its_core, its_y // 2 * 4 + cx)

    def remote(src, dst, send, recv, to):
        return pltpu.make_async_remote_copy(src, dst, send, recv, device_id=to, device_id_type=MESH)

    def cols(h):
        return pl.ds(pl.multiple_of(h * HEAD, HEAD), HEAD)

    @pl.loop(0, KV_HEADS)
    def _(g):
        pltpu.make_async_copy(k_in.at[:, cols(g)], kv.at[g, 0, 0], in_sem.at[6]).start()
        pltpu.make_async_copy(v_in.at[:, cols(g)], kv.at[g, 0, 1], in_sem.at[6]).start()

    pltpu.make_async_copy(x_in, x, in_sem.at[5]).start()
    pltpu.make_async_copy(len_in, lens, in_sem.at[0]).start()
    pltpu.make_async_copy(lse_in, lse, in_sem.at[1]).start()
    pltpu.make_async_copy(o_in, o, in_sem.at[4]).start()

    @pl.loop(0, HEADS)
    def _(h):
        pltpu.make_async_copy(do_in.at[:, cols(h)], do.at[h], in_sem.at[3]).start()
        pltpu.make_async_copy(q_in.at[:, cols(h)], q.at[h], in_sem.at[2]).start()

    barrier = pltpu.get_barrier_semaphore()

    @pl.loop(1, 8)
    def _(s):
        for to in (along_z(s), device(*member(s))):
            pl.semaphore_signal(barrier, inc=1, device_id=to, device_id_type=MESH)

    for s in range(1, 4):
        pl.semaphore_signal(barrier, inc=1, device_id=along_x(s), device_id_type=MESH)
    pl.semaphore_wait(barrier, 17)

    wait_for(kv.at[:, 0], in_sem.at[6])

    @pl.loop(0, KV_HEADS)
    def _(g):
        remote(kv.at[g, 0], kv.at[g, 1], kv_send, kv_recv.at[g, 1], y_partner).start()

    def send_along_x(g, source):
        for d in (1, 3, 2):
            remote(kv.at[g, source], kv.at[g, 2 * d + source], kv_send, kv_recv.at[g, 0], along_x(d)).start()

    def pass_on(g):
        wait_for(kv.at[g, 1], kv_recv.at[g, 1])
        send_along_x(g, 1)

    send_along_x(0, 0)
    send_along_x(1, 0)

    wait_for(x, in_sem.at[5])

    @pl.loop(0, DP)
    def _(b):
        xt[b // (2 * Z), b // 2 % Z, b % 2] = jnp.transpose(x[:, cols(b)]).reshape(2, 4, OUT_ROWS, ROWS)

    pltpu.make_async_copy(xt.at[y_lo, :, core, y_hi], xall.at[:, :, :, 0:ROWS], in_sem.at[7]).start()

    @pl.loop(1, 8)
    def _(s):
        its_core, its_y = member(s)
        mine = xt.at[its_y % 2, :, its_core, its_y // 2]
        remote(mine, xall.at[:, :, :, cols(s)], xt_send, xt_recv, device(its_core, its_y)).start()

    pass_on(0)
    send_along_x(2, 0)
    pass_on(1)
    send_along_x(3, 0)

    wait_for(lens, in_sem.at[0])
    end0 = lens[0, 0]
    end1 = end0 + lens[0, 1]
    end2 = end1 + lens[0, 2]
    end3 = end2 + lens[0, 3]
    query_pos = lax.broadcasted_iota(jnp.int32, (ROWS, ROWS), 1) * CTX + ctx
    first = jnp.zeros((ROWS, ROWS), jnp.int32)
    for end in (end0, end1, end2, end3):
        first = jnp.where(query_pos >= end, end, first)

    @pl.loop(0, CTX)
    def _(s):
        key_pos = lax.broadcasted_iota(jnp.int32, (ROWS, ROWS), 0) * CTX + behind(s)
        allowed = (key_pos >= first) & (key_pos <= query_pos)
        bias[s] = jnp.where(allowed, 0.0, -1e30).astype(F32)

    pass_on(2)
    wait_for(lse, in_sem.at[1])
    wait_for(o, in_sem.at[4])
    wait_for(do, in_sem.at[3])
    wait_for(q, in_sem.at[2])

    @pl.loop(0, KV_HEADS)
    def _(g):
        rows = []
        for h in range(GROUP):
            head = g * GROUP + h
            product = do[head].astype(F32) * o[:, cols(head)].astype(F32)
            rows.append(jnp.sum(jnp.transpose(product), axis=0, keepdims=True))
        delta[pl.ds(pl.multiple_of(g * GROUP, GROUP), GROUP), :] = jnp.concatenate(rows, axis=0)

    pass_on(3)

    def attend(g):
        wait_for(kv.at[g, 2:8], kv_recv.at[g, 0])
        heads = pl.ds(pl.multiple_of(g * GROUP, GROUP), GROUP)
        log2_totals = lse[heads, :] * LOG2E
        deltas = delta[heads, :]
        dqt[...] = jnp.zeros_like(dqt)

        @pl.loop(0, CTX * ROWS // KEYS)
        def _(t):
            blocks = pl.ds(t * (KEYS // ROWS), KEYS // ROWS)
            keys = kv[g, blocks, 0].reshape(KEYS, HEAD)
            values = kv[g, blocks, 1].reshape(KEYS, HEAD)
            queries = q[heads].reshape(GROUP * ROWS, HEAD)
            out_grads = do[heads].reshape(GROUP * ROWS, HEAD)
            seen = bias[blocks].reshape(KEYS, ROWS)
            scores = dot(keys, queries, (1, 1))
            grad_probs = dot(values, out_grads, (1, 1))
            for h in range(GROUP):
                at = slice(h * ROWS, (h + 1) * ROWS)
                probs = jnp.exp2(scores[:, at] * (SCALE * LOG2E) + (seen - log2_totals[h : h + 1, :]))
                pt[:, at] = probs.astype(BF16)
                dst[:, at] = (probs * (grad_probs[:, at] - deltas[h : h + 1, :])).astype(BF16)
            grad_scores = dst[...]
            dv = dot(pt[...], out_grads, (1, 0))
            dk = dot(grad_scores, queries, (1, 0)) * SCALE
            part[g, t, :, :, 0:HEAD] = dk.astype(BF16).reshape(2, ROWS, HEAD)
            part[g, t, :, :, HEAD:] = dv.astype(BF16).reshape(2, ROWS, HEAD)
            dqt[...] += dot(keys, grad_scores, (0, 0))

        @pl.when(g < Y_FIRST)
        def _():
            remote(part.at[g, :, 1], y_parts.at[g], p_send, p_recv.at[g], y_partner).start()

        @pl.when(g >= Y_FIRST)
        def _():
            for d in (1, 3, 2):
                remote(part.at[g, d], x_parts.at[g, d], p_send, p_recv.at[g], along_x(4 - d)).start()

        for h in range(GROUP):
            block = jnp.transpose(dqt[:, h * ROWS : (h + 1) * ROWS]) * SCALE
            dq_out[:, cols(g * GROUP + h)] = block.astype(BF16)

    def half_sums(g):
        @pl.when(g < Y_FIRST)
        def _():
            wait_for(y_parts.at[g], p_recv.at[g])
            owned[g] = part[g, 0, 0].astype(F32) + y_parts[g, 0].astype(F32)
            for d in (1, 3, 2):
                mids[g, d] = (part[g, d, 0].astype(F32) + y_parts[g, d].astype(F32)).astype(BF16)
                remote(mids.at[g, d], x_parts.at[g, d, 0], p_send, m_recv.at[g], along_x(4 - d)).start()

        @pl.when(g >= Y_FIRST)
        def _():
            wait_for(x_parts.at[g, 1:4], p_recv.at[g])
            other = part[g, 0, 1].astype(F32)
            for d in range(1, 4):
                other += x_parts[g, d, 1].astype(F32)
            mids[g, 0] = other.astype(BF16)
            remote(mids.at[g, 0], y_parts.at[g, 0], p_send, m_recv.at[g], y_partner).start()
            mine = part[g, 0, 0].astype(F32)
            for d in range(1, 4):
                mine += x_parts[g, d, 0].astype(F32)
            owned[g] = mine

    def gather_sums(g):
        @pl.when(g < Y_FIRST)
        def _():
            wait_for(x_parts.at[g, 1:4, 0], m_recv.at[g])
            total = owned[g]
            for d in range(1, 4):
                total += x_parts[g, d, 0].astype(F32)
            grads[g, 0] = total.astype(BF16)

        @pl.when(g >= Y_FIRST)
        def _():
            wait_for(y_parts.at[g, 0], m_recv.at[g])
            grads[g, 0] = (owned[g] + y_parts[g, 0].astype(F32)).astype(BF16)

        for s in range(1, 4):
            remote(grads.at[g, 0], grads.at[g, s], g_send, g_recv.at[g], device(*member(s))).start()
        remote(grads.at[g, 0], grads.at[g, 4], g_send, c_recv.at[g], device(*member(4))).start()

    def hand_over(g):
        wait_for(grads.at[g, 1:4], g_recv.at[g])
        remote(grads.at[g, 1:4], grads.at[g, 5:8], g_send, c_recv.at[g], device(*member(4))).start()

    def weigh(g):
        wait_for(grads.at[g, 4:8], c_recv.at[g])
        product = dot(xall[...].reshape(8 * 4 * OUT_ROWS, CTX * ROWS), grads[g].reshape(CTX * ROWS, 2 * HEAD), (1, 0))
        w[...] = product.reshape(Z, 4, OUT_ROWS, 2 * HEAD)
        x_out[g] = w[...].astype(BF16)
        for d in (1, 3, 2):
            to = along_x(d)
            remote(x_out.at[g, :, to[1] % 4], x_land.at[g, d], x_send, x_recv.at[g], to).start()
        x_acc[g] = w[:, cx]

    def sum_x(g):
        wait_for(x_land.at[g, 1:4], x_recv.at[g])
        total = x_acc[g]
        for d in range(1, 4):
            total += x_land[g, d].astype(F32)
        z_acc[g] = total
        z_out[g] = total.astype(BF16)

        @pl.loop(1, Z)
        def _(s):
            remote(z_out.at[g, (z + s) % Z], z_land.at[g, s], z_send, z_recv.at[g], along_z(s)).start()

    def sum_z(g):
        wait_for(z_land.at[g, 1:Z], z_recv.at[g])
        total = z_acc[g, z]
        for s in range(1, Z):
            total += z_land[g, s].astype(F32)
        kw_out[:, cols(g)] = total[:, 0:HEAD]
        vw_out[:, cols(g)] = total[:, HEAD:]

    stages = tuple(zip((sum_z, sum_x, hand_over, weigh, gather_sums, half_sums), (LAGS[k] for k in (5, 4, 2, 3, 1, 0))))

    @pl.loop(0, KV_HEADS + LAGS[5])
    def _(step):
        @pl.when(step < KV_HEADS)
        def _():
            attend(step)

        @pl.when(step == LAGS[3])
        def _():
            wait_for(xt.at[0, :, 0, 0], in_sem.at[7])
            wait_for(xall.at[:, :, :, ROWS:], xt_recv)

        for stage, lag in stages:

            @pl.when((step >= lag) & (step < KV_HEADS + lag))
            def _(stage=stage, lag=lag):
                stage(step - lag)

    wait_for(kv.at[:, 1:CTX], kv_send)
    wait_for(xall.at[:, :, :, ROWS:], xt_send)
    wait_for(grads.at[:, 1:8], p_send)
    wait_for(grads.at[:, 1:8], g_send)
    wait_for(x_land.at[:, 1:4], x_send)
    wait_for(z_land.at[:, 1:Z], z_send)


def local(normed_input, queries, keys, values, attention_output, log_totals, output_gradient, lengths):
    dma = pltpu.SemaphoreType.DMA
    vmem = pltpu.VMEM
    anywhere = pl.BlockSpec(memory_space=pl.ANY)
    shapes = (
        jax.ShapeDtypeStruct((ROWS, HEADS * HEAD), BF16),
        jax.ShapeDtypeStruct((OUT_ROWS, KV_HEADS * HEAD), F32),
        jax.ShapeDtypeStruct((OUT_ROWS, KV_HEADS * HEAD), F32),
    )
    return pl.pallas_call(
        kernel,
        out_shape=tuple(vmem(shape.shape, shape.dtype) for shape in shapes),
        in_specs=[anywhere] * 8,
        out_specs=(pl.BlockSpec(memory_space=vmem),) * 3,
        scratch_shapes=[
            pltpu.SMEM((1, 4), jnp.int32),
            vmem((HEADS, ROWS), F32),
            vmem((HEADS, ROWS), F32),
            vmem((HEADS, ROWS, HEAD), BF16),
            vmem((HEADS, ROWS, HEAD), BF16),
            vmem((ROWS, HEADS * HEAD), BF16),
            vmem((ROWS, DP * CTX * OUT_ROWS), BF16),
            vmem((2, Z, 2, 2, 4, OUT_ROWS, ROWS), BF16),
            vmem((Z, 4, OUT_ROWS, CTX * ROWS), BF16),
            vmem((KV_HEADS, CTX, 2, ROWS, HEAD), BF16),
            vmem((CTX, ROWS, ROWS), F32),
            vmem((KEYS, GROUP * ROWS), BF16),
            vmem((KEYS, GROUP * ROWS), BF16),
            vmem((HEAD, GROUP * ROWS), F32),
            vmem((KV_HEADS, 4, 2, ROWS, 2 * HEAD), BF16),
            vmem((KV_HEADS, 4, ROWS, 2 * HEAD), BF16),
            vmem((KV_HEADS, 4, 2, ROWS, 2 * HEAD), BF16),
            vmem((KV_HEADS, 4, ROWS, 2 * HEAD), BF16),
            vmem((KV_HEADS, ROWS, 2 * HEAD), F32),
            vmem((KV_HEADS, CTX, ROWS, 2 * HEAD), BF16),
            vmem((Z, 4, OUT_ROWS, 2 * HEAD), F32),
            vmem((KV_HEADS, Z, OUT_ROWS, 2 * HEAD), F32),
            vmem((KV_HEADS, Z, 4, OUT_ROWS, 2 * HEAD), BF16),
            vmem((KV_HEADS, 4, Z, OUT_ROWS, 2 * HEAD), BF16),
            vmem((KV_HEADS, Z, OUT_ROWS, 2 * HEAD), F32),
            vmem((KV_HEADS, Z, OUT_ROWS, 2 * HEAD), BF16),
            vmem((KV_HEADS, Z, OUT_ROWS, 2 * HEAD), BF16),
            dma((8,)),
            dma,
            dma((KV_HEADS, 2)),
            dma,
            dma,
            dma,
            dma((KV_HEADS,)),
            dma((KV_HEADS,)),
            dma,
            dma((KV_HEADS,)),
            dma((KV_HEADS,)),
            dma,
            dma((KV_HEADS,)),
            dma,
            dma((KV_HEADS,)),
        ],
        compiler_params=pltpu.CompilerParams(
            collective_id=0, has_side_effects=True, vmem_limit_bytes=56 * 2**20
        ),
    )(normed_input, queries, keys, values, attention_output, log_totals.T, output_gradient, lengths)

def solution(mesh):
    rows = P(("dp", "ctx"), None)
    return jax.shard_map(
        local,
        mesh=mesh,
        in_specs=(rows,) * 7 + (P("dp", None),),
        out_specs=(rows, rows, rows),
        check_vma=False,
    )
```

```python
import math

import jax
import jax.numpy as jnp
from jax import lax
from jax.experimental import pallas as pl
from jax.experimental.pallas import tpu as pltpu
from jax.sharding import PartitionSpec as P

KV_HEADS = 4
GROUP = 8
HEADS = KV_HEADS * GROUP
HEAD = 128
ROWS = 128
CTX = 8
DP = 32
LAGS = (1, 2, 3, 3, 4)
Z = 8
OUT_ROWS = 16
KEYS = 256
SCALE = 1.0 / math.sqrt(HEAD)
LOG2E = math.log2(math.e)
MESH = pl.DeviceIdType.MESH
F32, BF16 = jnp.float32, jnp.bfloat16


def wait_for(ref, sem):
    pltpu.make_async_copy(ref, ref, sem).wait()


def dot(a, b, contract):
    return lax.dot_general(a, b, ((contract[:1], contract[1:]), ((), ())), preferred_element_type=F32)


def kernel(
    x_in, q_in, k_in, v_in, o_in, lse_in, do_in, len_in,
    dq_out, kw_out, vw_out,
    lens, lse, delta, q, do, o, x, xt, xall, kv, bias, pt, dst, dqt, part, y_parts, x_parts, mids, owned, grads, w,
    x_acc, x_out, x_land, z_acc, z_out, z_land,
    in_sem, kv_send, kv_recv, xt_send, xt_recv, p_send, p_recv, m_recv, g_send, g_recv, c_recv,
    x_send, x_recv, z_send, z_recv,
):
    dp, ctx = lax.axis_index("dp"), lax.axis_index("ctx")
    y_hi, cx = ctx // 4, ctx % 4
    y_lo, z, core = dp // (2 * Z), dp // 2 % Z, dp % 2
    y = y_hi * 2 + y_lo

    def behind(s):
        return (y_hi + s % 2) % 2 * 4 + (cx + 4 - s // 2) % 4

    y_partner = (dp, (1 - y_hi) * 4 + cx)

    def along_z(s):
        return ((y_lo * Z + (z + s) % Z) * 2 + core, ctx)

    def along_x(s):
        return (dp, y_hi * 4 + (cx + s) % 4)

    def member(s):
        return (core + s // 4) % 2, (y + s % 4) % 4

    def device(its_core, its_y):
        return ((its_y % 2 * Z + z) * 2 + its_core, its_y // 2 * 4 + cx)

    def remote(src, dst, send, recv, to):
        return pltpu.make_async_remote_copy(src, dst, send, recv, device_id=to, device_id_type=MESH)

    def cols(h):
        return pl.ds(pl.multiple_of(h * HEAD, HEAD), HEAD)

    @pl.loop(0, KV_HEADS)
    def _(g):
        pltpu.make_async_copy(k_in.at[:, cols(g)], kv.at[g, 0, 0], in_sem.at[6]).start()
        pltpu.make_async_copy(v_in.at[:, cols(g)], kv.at[g, 0, 1], in_sem.at[6]).start()

    pltpu.make_async_copy(x_in, x, in_sem.at[5]).start()
    pltpu.make_async_copy(len_in, lens, in_sem.at[0]).start()
    pltpu.make_async_copy(lse_in, lse, in_sem.at[1]).start()
    pltpu.make_async_copy(o_in, o, in_sem.at[4]).start()

    @pl.loop(0, HEADS)
    def _(h):
        pltpu.make_async_copy(do_in.at[:, cols(h)], do.at[h], in_sem.at[3]).start()
        pltpu.make_async_copy(q_in.at[:, cols(h)], q.at[h], in_sem.at[2]).start()

    barrier = pltpu.get_barrier_semaphore()

    @pl.loop(1, 8)
    def _(s):
        for to in (along_z(s), device(*member(s))):
            pl.semaphore_signal(barrier, inc=1, device_id=to, device_id_type=MESH)

    for s in range(1, 4):
        pl.semaphore_signal(barrier, inc=1, device_id=along_x(s), device_id_type=MESH)
    pl.semaphore_wait(barrier, 17)

    wait_for(kv.at[:, 0], in_sem.at[6])

    @pl.loop(0, KV_HEADS)
    def _(g):
        remote(kv.at[g, 0], kv.at[g, 1], kv_send, kv_recv.at[g, 1], y_partner).start()

    def to_neighbours(g, source):
        remote(kv.at[g, source], kv.at[g, 2 + source], kv_send, kv_recv.at[g, 2], along_x(1)).start()
        remote(kv.at[g, source], kv.at[g, 6 + source], kv_send, kv_recv.at[g, 3], along_x(3)).start()

    def pass_partner(g):
        wait_for(kv.at[g, 1], kv_recv.at[g, 1])
        to_neighbours(g, 1)

    def pass_halves(g):
        wait_for(kv.at[g, 2:4], kv_recv.at[g, 2])
        remote(kv.at[g, 2:4, 0], kv.at[g, 4:6, 0], kv_send, kv_recv.at[g, 0], along_x(1)).start()
        wait_for(kv.at[g, 6:8], kv_recv.at[g, 3])
        remote(kv.at[g, 6:8, 1], kv.at[g, 4:6, 1], kv_send, kv_recv.at[g, 0], along_x(3)).start()

    to_neighbours(0, 0)
    to_neighbours(1, 0)

    wait_for(x, in_sem.at[5])

    @pl.loop(0, DP)
    def _(b):
        xt[b // (2 * Z), b // 2 % Z, b % 2] = jnp.transpose(x[:, cols(b)]).reshape(2, 4, OUT_ROWS, ROWS)

    pltpu.make_async_copy(xt.at[y_lo, :, core, y_hi], xall.at[:, :, :, 0:ROWS], in_sem.at[7]).start()

    @pl.loop(1, 8)
    def _(s):
        its_core, its_y = member(s)
        mine = xt.at[its_y % 2, :, its_core, its_y // 2]
        remote(mine, xall.at[:, :, :, cols(s)], xt_send, xt_recv, device(its_core, its_y)).start()

    pass_partner(0)
    pass_partner(1)
    to_neighbours(2, 0)

    wait_for(lens, in_sem.at[0])
    end0 = lens[0, 0]
    end1 = end0 + lens[0, 1]
    end2 = end1 + lens[0, 2]
    end3 = end2 + lens[0, 3]
    query_pos = lax.broadcasted_iota(jnp.int32, (ROWS, ROWS), 1) * CTX + ctx
    first = jnp.zeros((ROWS, ROWS), jnp.int32)
    for end in (end0, end1, end2, end3):
        first = jnp.where(query_pos >= end, end, first)

    @pl.loop(0, CTX)
    def _(s):
        key_pos = lax.broadcasted_iota(jnp.int32, (ROWS, ROWS), 0) * CTX + behind(s)
        allowed = (key_pos >= first) & (key_pos <= query_pos)
        bias[s] = jnp.where(allowed, 0.0, -1e30).astype(F32)

    pass_halves(0)
    pass_partner(2)
    to_neighbours(3, 0)
    wait_for(lse, in_sem.at[1])
    wait_for(o, in_sem.at[4])
    wait_for(do, in_sem.at[3])
    wait_for(q, in_sem.at[2])

    @pl.loop(0, KV_HEADS)
    def _(g):
        rows = []
        for h in range(GROUP):
            head = g * GROUP + h
            product = do[head].astype(F32) * o[:, cols(head)].astype(F32)
            rows.append(jnp.sum(jnp.transpose(product), axis=0, keepdims=True))
        delta[pl.ds(pl.multiple_of(g * GROUP, GROUP), GROUP), :] = jnp.concatenate(rows, axis=0)

    pass_partner(3)
    pass_halves(1)

    def attend(g):
        wait_for(kv.at[g, 4:6], kv_recv.at[g, 0])
        heads = pl.ds(pl.multiple_of(g * GROUP, GROUP), GROUP)
        log2_totals = lse[heads, :] * LOG2E
        deltas = delta[heads, :]
        dqt[...] = jnp.zeros_like(dqt)

        @pl.loop(0, CTX * ROWS // KEYS)
        def _(t):
            blocks = pl.ds(t * (KEYS // ROWS), KEYS // ROWS)
            keys = kv[g, blocks, 0].reshape(KEYS, HEAD)
            values = kv[g, blocks, 1].reshape(KEYS, HEAD)
            queries = q[heads].reshape(GROUP * ROWS, HEAD)
            out_grads = do[heads].reshape(GROUP * ROWS, HEAD)
            seen = bias[blocks].reshape(KEYS, ROWS)
            scores = dot(keys, queries, (1, 1))
            grad_probs = dot(values, out_grads, (1, 1))
            for h in range(GROUP):
                at = slice(h * ROWS, (h + 1) * ROWS)
                probs = jnp.exp2(scores[:, at] * (SCALE * LOG2E) + (seen - log2_totals[h : h + 1, :]))
                pt[:, at] = probs.astype(BF16)
                dst[:, at] = (probs * (grad_probs[:, at] - deltas[h : h + 1, :])).astype(BF16)
            grad_scores = dst[...]
            dv = dot(pt[...], out_grads, (1, 0))
            dk = dot(grad_scores, queries, (1, 0)) * SCALE
            part[g, t, :, :, 0:HEAD] = dk.astype(BF16).reshape(2, ROWS, HEAD)
            part[g, t, :, :, HEAD:] = dv.astype(BF16).reshape(2, ROWS, HEAD)
            dqt[...] += dot(keys, grad_scores, (0, 0))

            @pl.when((g == 0) & (t == 1))
            def _():
                pass_halves(2)

        for d in (1, 3, 2):
            remote(part.at[g, d], x_parts.at[g, d], p_send, p_recv.at[g], along_x(4 - d)).start()

        for h in range(GROUP):
            block = jnp.transpose(dqt[:, h * ROWS : (h + 1) * ROWS]) * SCALE
            dq_out[:, cols(g * GROUP + h)] = block.astype(BF16)

    def half_sums(g):
        wait_for(x_parts.at[g, 1:4], p_recv.at[g])
        other = part[g, 0, 1].astype(F32)
        for d in range(1, 4):
            other += x_parts[g, d, 1].astype(F32)
        mids[g] = other.astype(BF16)
        remote(mids.at[g], y_parts.at[g], p_send, m_recv.at[g], y_partner).start()
        mine = part[g, 0, 0].astype(F32)
        for d in range(1, 4):
            mine += x_parts[g, d, 0].astype(F32)
        owned[g] = mine

    def gather_sums(g):
        wait_for(y_parts.at[g], m_recv.at[g])
        grads[g, 0] = (owned[g] + y_parts[g].astype(F32)).astype(BF16)
        for s in range(1, 4):
            remote(grads.at[g, 0], grads.at[g, s], g_send, g_recv.at[g], device(*member(s))).start()
        remote(grads.at[g, 0], grads.at[g, 4], g_send, c_recv.at[g], device(*member(4))).start()

    def hand_over(g):
        wait_for(grads.at[g, 1:4], g_recv.at[g])
        remote(grads.at[g, 1:4], grads.at[g, 5:8], g_send, c_recv.at[g], device(*member(4))).start()

    def weigh(g):
        wait_for(grads.at[g, 4:8], c_recv.at[g])
        product = dot(xall[...].reshape(8 * 4 * OUT_ROWS, CTX * ROWS), grads[g].reshape(CTX * ROWS, 2 * HEAD), (1, 0))
        w[...] = product.reshape(Z, 4, OUT_ROWS, 2 * HEAD)
        x_out[g] = w[...].astype(BF16)
        for d in (1, 3, 2):
            to = along_x(d)
            remote(x_out.at[g, :, to[1] % 4], x_land.at[g, d], x_send, x_recv.at[g], to).start()
        x_acc[g] = w[:, cx]

    def sum_x(g):
        wait_for(x_land.at[g, 1:4], x_recv.at[g])
        total = x_acc[g]
        for d in range(1, 4):
            total += x_land[g, d].astype(F32)
        z_acc[g] = total
        z_out[g] = total.astype(BF16)

        @pl.loop(1, Z)
        def _(s):
            remote(z_out.at[g, (z + s) % Z], z_land.at[g, s], z_send, z_recv.at[g], along_z(s)).start()

    def sum_z(g):
        wait_for(z_land.at[g, 1:Z], z_recv.at[g])
        total = z_acc[g, z]
        for s in range(1, Z):
            total += z_land[g, s].astype(F32)
        kw_out[:, cols(g)] = total[:, 0:HEAD]
        vw_out[:, cols(g)] = total[:, HEAD:]

    stages = ((hand_over, LAGS[2]), (gather_sums, LAGS[1]), (sum_x, LAGS[4]), (weigh, LAGS[3]), (half_sums, LAGS[0]))

    @pl.loop(0, KV_HEADS + LAGS[4])
    def _(step):
        @pl.when(step == 1)
        def _():
            pass_halves(3)

        @pl.when(step < KV_HEADS)
        def _():
            attend(step)

        @pl.when(step == LAGS[3])
        def _():
            wait_for(xt.at[0, :, 0, 0], in_sem.at[7])
            wait_for(xall.at[:, :, :, ROWS:], xt_recv)

        for stage, lag in stages:

            @pl.when((step >= lag) & (step < KV_HEADS + lag))
            def _(stage=stage, lag=lag):
                stage(step - lag)

    @pl.loop(0, KV_HEADS)
    def _(g):
        sum_z(g)

    wait_for(kv.at[:, 1:CTX], kv_send)
    wait_for(xall.at[:, :, :, ROWS:], xt_send)
    wait_for(grads.at[:, 1:8], p_send)
    wait_for(grads.at[:, 1:8], g_send)
    wait_for(x_land.at[:, 1:4], x_send)
    wait_for(z_land.at[:, 1:Z], z_send)


def local(normed_input, queries, keys, values, attention_output, log_totals, output_gradient, lengths):
    dma = pltpu.SemaphoreType.DMA
    vmem = pltpu.VMEM
    anywhere = pl.BlockSpec(memory_space=pl.ANY)
    shapes = (
        jax.ShapeDtypeStruct((ROWS, HEADS * HEAD), BF16),
        jax.ShapeDtypeStruct((OUT_ROWS, KV_HEADS * HEAD), F32),
        jax.ShapeDtypeStruct((OUT_ROWS, KV_HEADS * HEAD), F32),
    )
    return pl.pallas_call(
        kernel,
        out_shape=tuple(vmem(shape.shape, shape.dtype) for shape in shapes),
        in_specs=[anywhere] * 8,
        out_specs=(pl.BlockSpec(memory_space=vmem),) * 3,
        scratch_shapes=[
            pltpu.SMEM((1, 4), jnp.int32),
            vmem((HEADS, ROWS), F32),
            vmem((HEADS, ROWS), F32),
            vmem((HEADS, ROWS, HEAD), BF16),
            vmem((HEADS, ROWS, HEAD), BF16),
            vmem((ROWS, HEADS * HEAD), BF16),
            vmem((ROWS, DP * CTX * OUT_ROWS), BF16),
            vmem((2, Z, 2, 2, 4, OUT_ROWS, ROWS), BF16),
            vmem((Z, 4, OUT_ROWS, CTX * ROWS), BF16),
            vmem((KV_HEADS, CTX, 2, ROWS, HEAD), BF16),
            vmem((CTX, ROWS, ROWS), F32),
            vmem((KEYS, GROUP * ROWS), BF16),
            vmem((KEYS, GROUP * ROWS), BF16),
            vmem((HEAD, GROUP * ROWS), F32),
            vmem((KV_HEADS, 4, 2, ROWS, 2 * HEAD), BF16),
            vmem((KV_HEADS, ROWS, 2 * HEAD), BF16),
            vmem((KV_HEADS, 4, 2, ROWS, 2 * HEAD), BF16),
            vmem((KV_HEADS, ROWS, 2 * HEAD), BF16),
            vmem((KV_HEADS, ROWS, 2 * HEAD), F32),
            vmem((KV_HEADS, CTX, ROWS, 2 * HEAD), BF16),
            vmem((Z, 4, OUT_ROWS, 2 * HEAD), F32),
            vmem((KV_HEADS, Z, OUT_ROWS, 2 * HEAD), F32),
            vmem((KV_HEADS, Z, 4, OUT_ROWS, 2 * HEAD), BF16),
            vmem((KV_HEADS, 4, Z, OUT_ROWS, 2 * HEAD), BF16),
            vmem((KV_HEADS, Z, OUT_ROWS, 2 * HEAD), F32),
            vmem((KV_HEADS, Z, OUT_ROWS, 2 * HEAD), BF16),
            vmem((KV_HEADS, Z, OUT_ROWS, 2 * HEAD), BF16),
            dma((8,)),
            dma,
            dma((KV_HEADS, 4)),
            dma,
            dma,
            dma,
            dma((KV_HEADS,)),
            dma((KV_HEADS,)),
            dma,
            dma((KV_HEADS,)),
            dma((KV_HEADS,)),
            dma,
            dma((KV_HEADS,)),
            dma,
            dma((KV_HEADS,)),
        ],
        compiler_params=pltpu.CompilerParams(
            collective_id=0, has_side_effects=True, vmem_limit_bytes=56 * 2**20
        ),
    )(normed_input, queries, keys, values, attention_output, log_totals.T, output_gradient, lengths)

def solution(mesh):
    rows = P(("dp", "ctx"), None)
    return jax.shard_map(
        local,
        mesh=mesh,
        in_specs=(rows,) * 7 + (P("dp", None),),
        out_specs=(rows, rows, rows),
        check_vma=False,
    )
```

```python
import math

import jax
import jax.numpy as jnp
from jax import lax
from jax.experimental import pallas as pl
from jax.experimental.pallas import tpu as pltpu
from jax.sharding import PartitionSpec as P

KV_HEADS = 4
GROUP = 8
HEADS = KV_HEADS * GROUP
HEAD = 128
ROWS = 128
CTX = 8
DP = 32
LAGS = (1, 2, 3, 3, 4)
Z = 8
OUT_ROWS = 16
KEYS = 256
SCALE = 1.0 / math.sqrt(HEAD)
LOG2E = math.log2(math.e)
MESH = pl.DeviceIdType.MESH
F32, BF16 = jnp.float32, jnp.bfloat16


def wait_for(ref, sem):
    pltpu.make_async_copy(ref, ref, sem).wait()


def dot(a, b, contract):
    return lax.dot_general(a, b, ((contract[:1], contract[1:]), ((), ())), preferred_element_type=F32)


def kernel(
    x_in, q_in, k_in, v_in, o_in, lse_in, do_in, len_in,
    dq_out, kw_out, vw_out,
    lens, lse, delta, q, do, o, x, xt, xall, kv, bias, pt, dst, dqt, part, y_parts, x_parts, mids, owned, grads, w,
    x_acc, x_out, x_land, z_acc, z_out, z_land,
    in_sem, kv_send, kv_recv, xt_send, xt_recv, p_send, p_recv, m_recv, g_send, g_recv, c_recv,
    x_send, x_recv, z_send, z_recv,
):
    dp, ctx = lax.axis_index("dp"), lax.axis_index("ctx")
    y_hi, cx = ctx // 4, ctx % 4
    y_lo, z, core = dp // (2 * Z), dp // 2 % Z, dp % 2
    y = y_hi * 2 + y_lo

    def behind(s):
        return (y_hi + s % 2) % 2 * 4 + (cx + 4 - s // 2) % 4

    y_partner = (dp, (1 - y_hi) * 4 + cx)

    def along_z(s):
        return ((y_lo * Z + (z + s) % Z) * 2 + core, ctx)

    def along_x(s):
        return (dp, y_hi * 4 + (cx + s) % 4)

    def member(s):
        return (core + s // 4) % 2, (y + s % 4) % 4

    def device(its_core, its_y):
        return ((its_y % 2 * Z + z) * 2 + its_core, its_y // 2 * 4 + cx)

    def remote(src, dst, send, recv, to):
        return pltpu.make_async_remote_copy(src, dst, send, recv, device_id=to, device_id_type=MESH)

    def cols(h):
        return pl.ds(pl.multiple_of(h * HEAD, HEAD), HEAD)

    @pl.loop(0, KV_HEADS)
    def _(g):
        pltpu.make_async_copy(k_in.at[:, cols(g)], kv.at[g, 0, 0], in_sem.at[6]).start()
        pltpu.make_async_copy(v_in.at[:, cols(g)], kv.at[g, 0, 1], in_sem.at[6]).start()

    pltpu.make_async_copy(x_in, x, in_sem.at[5]).start()
    pltpu.make_async_copy(len_in, lens, in_sem.at[0]).start()
    pltpu.make_async_copy(lse_in, lse, in_sem.at[1]).start()
    pltpu.make_async_copy(o_in, o, in_sem.at[4]).start()

    @pl.loop(0, HEADS)
    def _(h):
        pltpu.make_async_copy(do_in.at[:, cols(h)], do.at[h], in_sem.at[3]).start()
        pltpu.make_async_copy(q_in.at[:, cols(h)], q.at[h], in_sem.at[2]).start()

    barrier = pltpu.get_barrier_semaphore()

    @pl.loop(1, 8)
    def _(s):
        for to in (along_z(s), device(*member(s))):
            pl.semaphore_signal(barrier, inc=1, device_id=to, device_id_type=MESH)

    for s in range(1, 4):
        pl.semaphore_signal(barrier, inc=1, device_id=along_x(s), device_id_type=MESH)
    pl.semaphore_wait(barrier, 17)

    wait_for(kv.at[:, 0], in_sem.at[6])

    @pl.loop(0, KV_HEADS)
    def _(g):
        remote(kv.at[g, 0], kv.at[g, 1], kv_send, kv_recv.at[g, 1], y_partner).start()

    def to_neighbours(g, source):
        remote(kv.at[g, source], kv.at[g, 2 + source], kv_send, kv_recv.at[g, 2], along_x(1)).start()
        remote(kv.at[g, source], kv.at[g, 6 + source], kv_send, kv_recv.at[g, 3], along_x(3)).start()

    def pass_partner(g):
        wait_for(kv.at[g, 1], kv_recv.at[g, 1])
        to_neighbours(g, 1)

    def pass_halves(g):
        wait_for(kv.at[g, 2:4], kv_recv.at[g, 2])
        remote(kv.at[g, 2:4, 0], kv.at[g, 4:6, 0], kv_send, kv_recv.at[g, 0], along_x(1)).start()
        wait_for(kv.at[g, 6:8], kv_recv.at[g, 3])
        remote(kv.at[g, 6:8, 1], kv.at[g, 4:6, 1], kv_send, kv_recv.at[g, 0], along_x(3)).start()

    to_neighbours(0, 0)
    to_neighbours(1, 0)

    wait_for(x, in_sem.at[5])

    @pl.loop(0, DP)
    def _(b):
        xt[b // (2 * Z), b // 2 % Z, b % 2] = jnp.transpose(x[:, cols(b)]).reshape(2, 4, OUT_ROWS, ROWS)

    pltpu.make_async_copy(xt.at[y_lo, :, core, y_hi], xall.at[:, :, :, 0:ROWS], in_sem.at[7]).start()

    pass_partner(0)
    pass_partner(1)
    to_neighbours(2, 0)

    wait_for(lens, in_sem.at[0])
    end0 = lens[0, 0]
    end1 = end0 + lens[0, 1]
    end2 = end1 + lens[0, 2]
    end3 = end2 + lens[0, 3]
    query_pos = lax.broadcasted_iota(jnp.int32, (ROWS, ROWS), 1) * CTX + ctx
    first = jnp.zeros((ROWS, ROWS), jnp.int32)
    for end in (end0, end1, end2, end3):
        first = jnp.where(query_pos >= end, end, first)

    @pl.loop(0, CTX)
    def _(s):
        key_pos = lax.broadcasted_iota(jnp.int32, (ROWS, ROWS), 0) * CTX + behind(s)
        allowed = (key_pos >= first) & (key_pos <= query_pos)
        bias[s] = jnp.where(allowed, 0.0, -1e30).astype(F32)

    pass_halves(0)
    pass_partner(2)
    to_neighbours(3, 0)
    wait_for(lse, in_sem.at[1])
    wait_for(o, in_sem.at[4])
    wait_for(do, in_sem.at[3])
    wait_for(q, in_sem.at[2])

    @pl.loop(0, KV_HEADS)
    def _(g):
        rows = []
        for h in range(GROUP):
            head = g * GROUP + h
            product = do[head].astype(F32) * o[:, cols(head)].astype(F32)
            rows.append(jnp.sum(jnp.transpose(product), axis=0, keepdims=True))
        delta[pl.ds(pl.multiple_of(g * GROUP, GROUP), GROUP), :] = jnp.concatenate(rows, axis=0)

    pass_partner(3)

    @pl.loop(1, 8)
    def _(s):
        its_core, its_y = member(s)
        mine = xt.at[its_y % 2, :, its_core, its_y // 2]
        remote(mine, xall.at[:, :, :, cols(s)], xt_send, xt_recv, device(its_core, its_y)).start()

    pass_halves(1)

    def attend(g):
        wait_for(kv.at[g, 4:6], kv_recv.at[g, 0])
        heads = pl.ds(pl.multiple_of(g * GROUP, GROUP), GROUP)
        log2_totals = lse[heads, :] * LOG2E
        deltas = delta[heads, :]
        dqt[...] = jnp.zeros_like(dqt)

        @pl.loop(0, CTX * ROWS // KEYS)
        def _(t):
            blocks = pl.ds(t * (KEYS // ROWS), KEYS // ROWS)
            keys = kv[g, blocks, 0].reshape(KEYS, HEAD)
            values = kv[g, blocks, 1].reshape(KEYS, HEAD)
            queries = q[heads].reshape(GROUP * ROWS, HEAD)
            out_grads = do[heads].reshape(GROUP * ROWS, HEAD)
            seen = bias[blocks].reshape(KEYS, ROWS)
            scores = dot(keys, queries, (1, 1))
            grad_probs = dot(values, out_grads, (1, 1))
            for h in range(GROUP):
                at = slice(h * ROWS, (h + 1) * ROWS)
                probs = jnp.exp2(scores[:, at] * (SCALE * LOG2E) + (seen - log2_totals[h : h + 1, :]))
                pt[:, at] = probs.astype(BF16)
                dst[:, at] = (probs * (grad_probs[:, at] - deltas[h : h + 1, :])).astype(BF16)
            grad_scores = dst[...]
            dv = dot(pt[...], out_grads, (1, 0))
            dk = dot(grad_scores, queries, (1, 0)) * SCALE
            part[g, t, :, :, 0:HEAD] = dk.astype(BF16).reshape(2, ROWS, HEAD)
            part[g, t, :, :, HEAD:] = dv.astype(BF16).reshape(2, ROWS, HEAD)
            dqt[...] += dot(keys, grad_scores, (0, 0))

            @pl.when((g == 0) & (t == 1))
            def _():
                pass_halves(2)

        for d in (1, 3, 2):
            remote(part.at[g, d], x_parts.at[g, d], p_send, p_recv.at[g], along_x(4 - d)).start()

        for h in range(GROUP):
            block = jnp.transpose(dqt[:, h * ROWS : (h + 1) * ROWS]) * SCALE
            dq_out[:, cols(g * GROUP + h)] = block.astype(BF16)

    def half_sums(g):
        wait_for(x_parts.at[g, 1:4], p_recv.at[g])
        other = part[g, 0, 1].astype(F32)
        for d in range(1, 4):
            other += x_parts[g, d, 1].astype(F32)
        mids[g] = other.astype(BF16)
        remote(mids.at[g], y_parts.at[g], p_send, m_recv.at[g], y_partner).start()
        mine = part[g, 0, 0].astype(F32)
        for d in range(1, 4):
            mine += x_parts[g, d, 0].astype(F32)
        owned[g] = mine

    def gather_sums(g):
        wait_for(y_parts.at[g], m_recv.at[g])
        grads[g, 0] = (owned[g] + y_parts[g].astype(F32)).astype(BF16)
        for s in (2, 1, 3):
            remote(grads.at[g, 0], grads.at[g, s], g_send, g_recv.at[g], device(*member(s))).start()
        remote(grads.at[g, 0], grads.at[g, 4], g_send, c_recv.at[g], device(*member(4))).start()

    def hand_over(g):
        wait_for(grads.at[g, 1:4], g_recv.at[g])
        remote(grads.at[g, 1:4], grads.at[g, 5:8], g_send, c_recv.at[g], device(*member(4))).start()

    def weigh(g):
        wait_for(grads.at[g, 4:8], c_recv.at[g])
        product = dot(xall[...].reshape(8 * 4 * OUT_ROWS, CTX * ROWS), grads[g].reshape(CTX * ROWS, 2 * HEAD), (1, 0))
        w[...] = product.reshape(Z, 4, OUT_ROWS, 2 * HEAD)
        x_out[g] = w[...].astype(BF16)
        for d in (1, 3, 2):
            to = along_x(d)
            remote(x_out.at[g, :, to[1] % 4], x_land.at[g, d], x_send, x_recv.at[g], to).start()
        x_acc[g] = w[:, cx]

    def sum_x(g):
        wait_for(x_land.at[g, 1:4], x_recv.at[g])
        total = x_acc[g]
        for d in range(1, 4):
            total += x_land[g, d].astype(F32)
        z_acc[g] = total
        z_out[g] = total.astype(BF16)

        @pl.loop(1, Z)
        def _(s):
            remote(z_out.at[g, (z + s) % Z], z_land.at[g, s], z_send, z_recv.at[g], along_z(s)).start()

    def sum_z(g):
        wait_for(z_land.at[g, 1:Z], z_recv.at[g])
        total = z_acc[g, z]
        for s in range(1, Z):
            total += z_land[g, s].astype(F32)
        kw_out[:, cols(g)] = total[:, 0:HEAD]
        vw_out[:, cols(g)] = total[:, HEAD:]

    stages = ((hand_over, LAGS[2]), (gather_sums, LAGS[1]), (weigh, LAGS[3]), (sum_x, LAGS[4]), (half_sums, LAGS[0]))

    @pl.loop(0, KV_HEADS + LAGS[4])
    def _(step):
        @pl.when(step == 1)
        def _():
            pass_halves(3)

        @pl.when(step < KV_HEADS)
        def _():
            attend(step)

        @pl.when(step == LAGS[3])
        def _():
            wait_for(xt.at[0, :, 0, 0], in_sem.at[7])
            wait_for(xall.at[:, :, :, ROWS:], xt_recv)

        for stage, lag in stages:

            @pl.when((step >= lag) & (step < KV_HEADS + lag))
            def _(stage=stage, lag=lag):
                stage(step - lag)

    @pl.loop(0, KV_HEADS)
    def _(g):
        sum_z(g)

    wait_for(kv.at[:, 1:CTX], kv_send)
    wait_for(xall.at[:, :, :, ROWS:], xt_send)
    wait_for(grads.at[:, 1:8], p_send)
    wait_for(grads.at[:, 1:8], g_send)
    wait_for(x_land.at[:, 1:4], x_send)
    wait_for(z_land.at[:, 1:Z], z_send)


def local(normed_input, queries, keys, values, attention_output, log_totals, output_gradient, lengths):
    dma = pltpu.SemaphoreType.DMA
    vmem = pltpu.VMEM
    anywhere = pl.BlockSpec(memory_space=pl.ANY)
    shapes = (
        jax.ShapeDtypeStruct((ROWS, HEADS * HEAD), BF16),
        jax.ShapeDtypeStruct((OUT_ROWS, KV_HEADS * HEAD), F32),
        jax.ShapeDtypeStruct((OUT_ROWS, KV_HEADS * HEAD), F32),
    )
    return pl.pallas_call(
        kernel,
        out_shape=tuple(vmem(shape.shape, shape.dtype) for shape in shapes),
        in_specs=[anywhere] * 8,
        out_specs=(pl.BlockSpec(memory_space=vmem),) * 3,
        scratch_shapes=[
            pltpu.SMEM((1, 4), jnp.int32),
            vmem((HEADS, ROWS), F32),
            vmem((HEADS, ROWS), F32),
            vmem((HEADS, ROWS, HEAD), BF16),
            vmem((HEADS, ROWS, HEAD), BF16),
            vmem((ROWS, HEADS * HEAD), BF16),
            vmem((ROWS, DP * CTX * OUT_ROWS), BF16),
            vmem((2, Z, 2, 2, 4, OUT_ROWS, ROWS), BF16),
            vmem((Z, 4, OUT_ROWS, CTX * ROWS), BF16),
            vmem((KV_HEADS, CTX, 2, ROWS, HEAD), BF16),
            vmem((CTX, ROWS, ROWS), F32),
            vmem((KEYS, GROUP * ROWS), BF16),
            vmem((KEYS, GROUP * ROWS), BF16),
            vmem((HEAD, GROUP * ROWS), F32),
            vmem((KV_HEADS, 4, 2, ROWS, 2 * HEAD), BF16),
            vmem((KV_HEADS, ROWS, 2 * HEAD), BF16),
            vmem((KV_HEADS, 4, 2, ROWS, 2 * HEAD), BF16),
            vmem((KV_HEADS, ROWS, 2 * HEAD), BF16),
            vmem((KV_HEADS, ROWS, 2 * HEAD), F32),
            vmem((KV_HEADS, CTX, ROWS, 2 * HEAD), BF16),
            vmem((Z, 4, OUT_ROWS, 2 * HEAD), F32),
            vmem((KV_HEADS, Z, OUT_ROWS, 2 * HEAD), F32),
            vmem((KV_HEADS, Z, 4, OUT_ROWS, 2 * HEAD), BF16),
            vmem((KV_HEADS, 4, Z, OUT_ROWS, 2 * HEAD), BF16),
            vmem((KV_HEADS, Z, OUT_ROWS, 2 * HEAD), F32),
            vmem((KV_HEADS, Z, OUT_ROWS, 2 * HEAD), BF16),
            vmem((KV_HEADS, Z, OUT_ROWS, 2 * HEAD), BF16),
            dma((8,)),
            dma,
            dma((KV_HEADS, 4)),
            dma,
            dma,
            dma,
            dma((KV_HEADS,)),
            dma((KV_HEADS,)),
            dma,
            dma((KV_HEADS,)),
            dma((KV_HEADS,)),
            dma,
            dma((KV_HEADS,)),
            dma,
            dma((KV_HEADS,)),
        ],
        compiler_params=pltpu.CompilerParams(
            collective_id=0, has_side_effects=True, vmem_limit_bytes=56 * 2**20
        ),
    )(normed_input, queries, keys, values, attention_output, log_totals.T, output_gradient, lengths)

def solution(mesh):
    rows = P(("dp", "ctx"), None)
    return jax.shard_map(
        local,
        mesh=mesh,
        in_specs=(rows,) * 7 + (P("dp", None),),
        out_specs=(rows, rows, rows),
        check_vma=False,
    )
```

```python
import math

import jax
import jax.numpy as jnp
from jax import lax
from jax.experimental import pallas as pl
from jax.experimental.pallas import tpu as pltpu
from jax.sharding import PartitionSpec as P

KV_HEADS = 4
GROUP = 8
HEADS = KV_HEADS * GROUP
HEAD = 128
ROWS = 128
CTX = 8
DP = 32
LAGS = (1, 2, 3, 3, 4)
Z = 8
OUT_ROWS = 16
KEYS = 256
SCALE = 1.0 / math.sqrt(HEAD)
LOG2E = math.log2(math.e)
MESH = pl.DeviceIdType.MESH
F32, BF16 = jnp.float32, jnp.bfloat16


def wait_for(ref, sem):
    pltpu.make_async_copy(ref, ref, sem).wait()


def dot(a, b, contract):
    return lax.dot_general(a, b, ((contract[:1], contract[1:]), ((), ())), preferred_element_type=F32)


def kernel(
    x_in, q_in, k_in, v_in, o_in, lse_in, do_in, len_in,
    dq_out, kw_out, vw_out,
    lens, lse, delta, q, do, o, x, xt, xall, kv, bias, pt, dst, dqt, part, y_parts, x_parts, mids, owned, grads, w,
    x_acc, x_out, x_land, z_acc, z_out, z_land,
    in_sem, kv_send, kv_recv, xt_send, xt_recv, p_send, p_recv, m_recv, g_send, g_recv, c_recv,
    x_send, x_recv, z_send, z_recv,
):
    dp, ctx = lax.axis_index("dp"), lax.axis_index("ctx")
    y_hi, cx = ctx // 4, ctx % 4
    y_lo, z, core = dp // (2 * Z), dp // 2 % Z, dp % 2
    y = y_hi * 2 + y_lo

    def behind(s):
        return (y_hi + s % 2) % 2 * 4 + (cx + 4 - s // 2) % 4

    y_partner = (dp, (1 - y_hi) * 4 + cx)

    def along_z(s):
        return ((y_lo * Z + (z + s) % Z) * 2 + core, ctx)

    def along_x(s):
        return (dp, y_hi * 4 + (cx + s) % 4)

    def member(s):
        return (core + s // 4) % 2, (y + s % 4) % 4

    def device(its_core, its_y):
        return ((its_y % 2 * Z + z) * 2 + its_core, its_y // 2 * 4 + cx)

    def remote(src, dst, send, recv, to):
        return pltpu.make_async_remote_copy(src, dst, send, recv, device_id=to, device_id_type=MESH)

    def cols(h):
        return pl.ds(pl.multiple_of(h * HEAD, HEAD), HEAD)

    @pl.loop(0, KV_HEADS)
    def _(g):
        pltpu.make_async_copy(k_in.at[:, cols(g)], kv.at[g, 0, 0], in_sem.at[6]).start()
        pltpu.make_async_copy(v_in.at[:, cols(g)], kv.at[g, 0, 1], in_sem.at[6]).start()

    pltpu.make_async_copy(x_in, x, in_sem.at[5]).start()
    pltpu.make_async_copy(len_in, lens, in_sem.at[0]).start()
    pltpu.make_async_copy(lse_in, lse, in_sem.at[1]).start()
    pltpu.make_async_copy(o_in, o, in_sem.at[4]).start()

    @pl.loop(0, HEADS)
    def _(h):
        pltpu.make_async_copy(do_in.at[:, cols(h)], do.at[h], in_sem.at[3]).start()
        pltpu.make_async_copy(q_in.at[:, cols(h)], q.at[h], in_sem.at[2]).start()

    barrier = pltpu.get_barrier_semaphore()

    @pl.loop(1, 8)
    def _(s):
        for to in (along_z(s), device(*member(s))):
            pl.semaphore_signal(barrier, inc=1, device_id=to, device_id_type=MESH)

    for s in range(1, 4):
        pl.semaphore_signal(barrier, inc=1, device_id=along_x(s), device_id_type=MESH)
    pl.semaphore_wait(barrier, 17)

    wait_for(kv.at[:, 0], in_sem.at[6])

    @pl.loop(0, KV_HEADS)
    def _(g):
        remote(kv.at[g, 0], kv.at[g, 1], kv_send, kv_recv.at[g, 1], y_partner).start()

    def to_neighbours(g, source):
        remote(kv.at[g, source], kv.at[g, 2 + source], kv_send, kv_recv.at[g, 2], along_x(1)).start()
        remote(kv.at[g, source], kv.at[g, 6 + source], kv_send, kv_recv.at[g, 3], along_x(3)).start()

    def pass_partner(g):
        wait_for(kv.at[g, 1], kv_recv.at[g, 1])
        to_neighbours(g, 1)

    def pass_halves(g):
        wait_for(kv.at[g, 2:4], kv_recv.at[g, 2])
        remote(kv.at[g, 2:4, 0], kv.at[g, 4:6, 0], kv_send, kv_recv.at[g, 0], along_x(1)).start()
        wait_for(kv.at[g, 6:8], kv_recv.at[g, 3])
        remote(kv.at[g, 6:8, 1], kv.at[g, 4:6, 1], kv_send, kv_recv.at[g, 0], along_x(3)).start()

    to_neighbours(0, 0)
    to_neighbours(1, 0)

    wait_for(x, in_sem.at[5])

    @pl.loop(0, DP)
    def _(b):
        xt[b // (2 * Z), b // 2 % Z, b % 2] = jnp.transpose(x[:, cols(b)]).reshape(2, 4, OUT_ROWS, ROWS)

    pltpu.make_async_copy(xt.at[y_lo, :, core, y_hi], xall.at[:, :, :, 0:ROWS], in_sem.at[7]).start()

    pass_partner(0)
    pass_partner(1)
    to_neighbours(2, 0)

    wait_for(lens, in_sem.at[0])
    end0 = lens[0, 0]
    end1 = end0 + lens[0, 1]
    end2 = end1 + lens[0, 2]
    end3 = end2 + lens[0, 3]
    query_pos = lax.broadcasted_iota(jnp.int32, (ROWS, ROWS), 1) * CTX + ctx
    first = jnp.zeros((ROWS, ROWS), jnp.int32)
    for end in (end0, end1, end2, end3):
        first = jnp.where(query_pos >= end, end, first)

    @pl.loop(0, CTX)
    def _(s):
        key_pos = lax.broadcasted_iota(jnp.int32, (ROWS, ROWS), 0) * CTX + behind(s)
        allowed = (key_pos >= first) & (key_pos <= query_pos)
        bias[s] = jnp.where(allowed, 0.0, -1e30).astype(F32)

    pass_halves(0)
    pass_partner(2)
    to_neighbours(3, 0)
    wait_for(lse, in_sem.at[1])
    wait_for(o, in_sem.at[4])
    wait_for(do, in_sem.at[3])
    wait_for(q, in_sem.at[2])

    @pl.loop(0, KV_HEADS)
    def _(g):
        rows = []
        for h in range(GROUP):
            head = g * GROUP + h
            product = do[head].astype(F32) * o[:, cols(head)].astype(F32)
            rows.append(jnp.sum(jnp.transpose(product), axis=0, keepdims=True))
        delta[pl.ds(pl.multiple_of(g * GROUP, GROUP), GROUP), :] = jnp.concatenate(rows, axis=0)

    pass_partner(3)

    @pl.loop(1, 8)
    def _(s):
        its_core, its_y = member(s)
        mine = xt.at[its_y % 2, :, its_core, its_y // 2]
        remote(mine, xall.at[:, :, :, cols(s)], xt_send, xt_recv, device(its_core, its_y)).start()

    pass_halves(1)

    def attend(g):
        wait_for(kv.at[g, 4:6], kv_recv.at[g, 0])
        heads = pl.ds(pl.multiple_of(g * GROUP, GROUP), GROUP)
        log2_totals = lse[heads, :] * LOG2E
        deltas = delta[heads, :]
        dqt[...] = jnp.zeros_like(dqt)

        @pl.loop(0, CTX * ROWS // KEYS)
        def _(t):
            blocks = pl.ds(t * (KEYS // ROWS), KEYS // ROWS)
            keys = kv[g, blocks, 0].reshape(KEYS, HEAD)
            values = kv[g, blocks, 1].reshape(KEYS, HEAD)
            queries = q[heads].reshape(GROUP * ROWS, HEAD)
            out_grads = do[heads].reshape(GROUP * ROWS, HEAD)
            seen = bias[blocks].reshape(KEYS, ROWS)
            scores = dot(keys, queries, (1, 1))
            grad_probs = dot(values, out_grads, (1, 1))
            for h in range(GROUP):
                at = slice(h * ROWS, (h + 1) * ROWS)
                probs = jnp.exp2(scores[:, at] * (SCALE * LOG2E) + (seen - log2_totals[h : h + 1, :]))
                pt[:, at] = probs.astype(BF16)
                dst[:, at] = (probs * (grad_probs[:, at] - deltas[h : h + 1, :])).astype(BF16)
            grad_scores = dst[...]
            dv = dot(pt[...], out_grads, (1, 0))
            dk = dot(grad_scores, queries, (1, 0)) * SCALE
            part[g, t, :, :, 0:HEAD] = dk.astype(BF16).reshape(2, ROWS, HEAD)
            part[g, t, :, :, HEAD:] = dv.astype(BF16).reshape(2, ROWS, HEAD)
            dqt[...] += dot(keys, grad_scores, (0, 0))

            @pl.when((g == 0) & (t == 1))
            def _():
                pass_halves(2)

        for d in (1, 3, 2):
            remote(part.at[g, d], x_parts.at[g, d], p_send, p_recv.at[g], along_x(4 - d)).start()

    def write_query_gradient(g):
        for h in range(GROUP):
            block = jnp.transpose(dqt[:, h * ROWS : (h + 1) * ROWS]) * SCALE
            dq_out[:, cols(g * GROUP + h)] = block.astype(BF16)

    def half_sums(g):
        wait_for(x_parts.at[g, 1:4], p_recv.at[g])
        other = part[g, 0, 1].astype(F32)
        for d in range(1, 4):
            other += x_parts[g, d, 1].astype(F32)
        mids[g] = other.astype(BF16)
        remote(mids.at[g], y_parts.at[g], p_send, m_recv.at[g], y_partner).start()
        mine = part[g, 0, 0].astype(F32)
        for d in range(1, 4):
            mine += x_parts[g, d, 0].astype(F32)
        owned[g] = mine

    def gather_sums(g):
        wait_for(y_parts.at[g], m_recv.at[g])
        grads[g, 0] = (owned[g] + y_parts[g].astype(F32)).astype(BF16)
        for s in (2, 1, 3):
            remote(grads.at[g, 0], grads.at[g, s], g_send, g_recv.at[g], device(*member(s))).start()
        remote(grads.at[g, 0], grads.at[g, 4], g_send, c_recv.at[g], device(*member(4))).start()

    def hand_over(g):
        wait_for(grads.at[g, 1:4], g_recv.at[g])
        remote(grads.at[g, 1:4], grads.at[g, 5:8], g_send, c_recv.at[g], device(*member(4))).start()

    def weigh(g):
        wait_for(grads.at[g, 4:8], c_recv.at[g])
        product = dot(xall[...].reshape(8 * 4 * OUT_ROWS, CTX * ROWS), grads[g].reshape(CTX * ROWS, 2 * HEAD), (1, 0))
        w[...] = product.reshape(Z, 4, OUT_ROWS, 2 * HEAD)
        x_out[g] = w[...].astype(BF16)
        for d in (1, 3, 2):
            to = along_x(d)
            remote(x_out.at[g, :, to[1] % 4], x_land.at[g, d], x_send, x_recv.at[g], to).start()
        x_acc[g] = w[:, cx]

    def sum_x(g):
        wait_for(x_land.at[g, 1:4], x_recv.at[g])
        total = x_acc[g]
        for d in range(1, 4):
            total += x_land[g, d].astype(F32)
        z_acc[g] = total
        z_out[g] = total.astype(BF16)

        @pl.loop(1, Z)
        def _(s):
            remote(z_out.at[g, (z + s) % Z], z_land.at[g, s], z_send, z_recv.at[g], along_z(s)).start()

    def sum_z(g):
        wait_for(z_land.at[g, 1:Z], z_recv.at[g])
        total = z_acc[g, z]
        for s in range(1, Z):
            total += z_land[g, s].astype(F32)
        kw_out[:, cols(g)] = total[:, 0:HEAD]
        vw_out[:, cols(g)] = total[:, HEAD:]

    stages = ((hand_over, LAGS[2]), (gather_sums, LAGS[1]), (weigh, LAGS[3]), (sum_x, LAGS[4]), (half_sums, LAGS[0]))

    @pl.loop(0, KV_HEADS + LAGS[4])
    def _(step):
        @pl.when(step == 1)
        def _():
            pass_halves(3)

        @pl.when(step < KV_HEADS)
        def _():
            attend(step)

        @pl.when(step == LAGS[3])
        def _():
            wait_for(xt.at[0, :, 0, 0], in_sem.at[7])
            wait_for(xall.at[:, :, :, ROWS:], xt_recv)

        for stage, lag in stages:

            @pl.when((step >= lag) & (step < KV_HEADS + lag))
            def _(stage=stage, lag=lag):
                stage(step - lag)

        @pl.when(step < KV_HEADS)
        def _():
            write_query_gradient(step)

    @pl.loop(0, KV_HEADS)
    def _(g):
        sum_z(g)

    wait_for(kv.at[:, 1:CTX], kv_send)
    wait_for(xall.at[:, :, :, ROWS:], xt_send)
    wait_for(grads.at[:, 1:8], p_send)
    wait_for(grads.at[:, 1:8], g_send)
    wait_for(x_land.at[:, 1:4], x_send)
    wait_for(z_land.at[:, 1:Z], z_send)


def local(normed_input, queries, keys, values, attention_output, log_totals, output_gradient, lengths):
    dma = pltpu.SemaphoreType.DMA
    vmem = pltpu.VMEM
    anywhere = pl.BlockSpec(memory_space=pl.ANY)
    shapes = (
        jax.ShapeDtypeStruct((ROWS, HEADS * HEAD), BF16),
        jax.ShapeDtypeStruct((OUT_ROWS, KV_HEADS * HEAD), F32),
        jax.ShapeDtypeStruct((OUT_ROWS, KV_HEADS * HEAD), F32),
    )
    return pl.pallas_call(
        kernel,
        out_shape=tuple(vmem(shape.shape, shape.dtype) for shape in shapes),
        in_specs=[anywhere] * 8,
        out_specs=(pl.BlockSpec(memory_space=vmem),) * 3,
        scratch_shapes=[
            pltpu.SMEM((1, 4), jnp.int32),
            vmem((HEADS, ROWS), F32),
            vmem((HEADS, ROWS), F32),
            vmem((HEADS, ROWS, HEAD), BF16),
            vmem((HEADS, ROWS, HEAD), BF16),
            vmem((ROWS, HEADS * HEAD), BF16),
            vmem((ROWS, DP * CTX * OUT_ROWS), BF16),
            vmem((2, Z, 2, 2, 4, OUT_ROWS, ROWS), BF16),
            vmem((Z, 4, OUT_ROWS, CTX * ROWS), BF16),
            vmem((KV_HEADS, CTX, 2, ROWS, HEAD), BF16),
            vmem((CTX, ROWS, ROWS), F32),
            vmem((KEYS, GROUP * ROWS), BF16),
            vmem((KEYS, GROUP * ROWS), BF16),
            vmem((HEAD, GROUP * ROWS), F32),
            vmem((KV_HEADS, 4, 2, ROWS, 2 * HEAD), BF16),
            vmem((KV_HEADS, ROWS, 2 * HEAD), BF16),
            vmem((KV_HEADS, 4, 2, ROWS, 2 * HEAD), BF16),
            vmem((KV_HEADS, ROWS, 2 * HEAD), BF16),
            vmem((KV_HEADS, ROWS, 2 * HEAD), F32),
            vmem((KV_HEADS, CTX, ROWS, 2 * HEAD), BF16),
            vmem((Z, 4, OUT_ROWS, 2 * HEAD), F32),
            vmem((KV_HEADS, Z, OUT_ROWS, 2 * HEAD), F32),
            vmem((KV_HEADS, Z, 4, OUT_ROWS, 2 * HEAD), BF16),
            vmem((KV_HEADS, 4, Z, OUT_ROWS, 2 * HEAD), BF16),
            vmem((KV_HEADS, Z, OUT_ROWS, 2 * HEAD), F32),
            vmem((KV_HEADS, Z, OUT_ROWS, 2 * HEAD), BF16),
            vmem((KV_HEADS, Z, OUT_ROWS, 2 * HEAD), BF16),
            dma((8,)),
            dma,
            dma((KV_HEADS, 4)),
            dma,
            dma,
            dma,
            dma((KV_HEADS,)),
            dma((KV_HEADS,)),
            dma,
            dma((KV_HEADS,)),
            dma((KV_HEADS,)),
            dma,
            dma((KV_HEADS,)),
            dma,
            dma((KV_HEADS,)),
        ],
        compiler_params=pltpu.CompilerParams(
            collective_id=0, has_side_effects=True, vmem_limit_bytes=56 * 2**20
        ),
    )(normed_input, queries, keys, values, attention_output, log_totals.T, output_gradient, lengths)

def solution(mesh):
    rows = P(("dp", "ctx"), None)
    return jax.shard_map(
        local,
        mesh=mesh,
        in_specs=(rows,) * 7 + (P("dp", None),),
        out_specs=(rows, rows, rows),
        check_vma=False,
    )
```
